128 devices in a mesh: gz: 8 (over z, x_lo), gy: 16 (over y, x_hi, core).
Axes of the slice: x: 4 (x_hi: 2, x_lo: 2; x = x_hi * 2 + x_lo), y: 4, z: 4, core: 2. Of those that a mesh axis runs over, the one named last changes fastest.
Arguments:
- prior: float32 [8, 128, 512, 256], P(None, 'gz', 'gy'), may hold values from 0 to 1
- levels: int32 [3, 128, 512, 256], P(None, 'gz', 'gy'), may hold values from 0 to 255
- seeds: int32 [128, 512, 256], P('gz', 'gy'), may hold values from 0 to 8, as said below
- bclass: int32 [8, 16], P('gz', 'gy'), may hold values from 0 to 3
Outputs:
- probs: float32 [8, 128, 512, 256], P(None, 'gz', 'gy')
The draws below stay inside these ranges and needn't reach their ends.
Inputs may be any that keep to these rules, and one draw needn't show every extreme that they name: `seeds`: 0 marks an unseeded voxel; k >= 1 fixes the voxel to label k - 1.
All inputs are finite; a program needn't handle non-finite values.
Results may differ from the reference program's by a relative error of at most 0.0003.
Values sent between devices are 32-bit elements; how exact they have to be, the bound alone decides.
No kernel may reach another device: no remote copies, remote signals or barrier semaphores. Data moves between devices by JAX's collectives and lax.ppermute only.
A program may use at most 64 MiB of HBM per device.

```python
import jax
import jax.numpy as jnp
from jax import lax

LABELS = 8
OUTER = 2
SWEEPS = 2
CZ = 16
CY = 32
CX = 256
NZ = 128
NY = 512
N_GZ = 8
N_GY = 16


def draw_seeds(key, part):
    first, second = jax.random.split(key)
    hits = jax.random.randint(first, (NZ, NY, CX), 0, 16)
    labels = jax.random.randint(second, (NZ, NY, CX), 1, LABELS + 1)
    return jnp.where(hits == 0, labels, 0).astype(jnp.int32)


def plant(drawn, rng, smallest, largest):
    spot = [jax.random.randint(jax.random.fold_in(rng, axis), (), 0, length) for axis, length in enumerate(drawn.shape)]
    longest = drawn.shape.index(max(drawn.shape))
    next_to = spot[:longest] + [(spot[longest] + 1) % drawn.shape[longest]] + spot[longest + 1:]
    return drawn.at[tuple(spot)].set(smallest).at[tuple(next_to)].set(largest)


def block_scale(key, dims, cuts, smallest, high):
    def one(axis_at, parts):
        steps = jax.random.uniform(jax.random.fold_in(jax.random.fold_in(key, 6), axis_at), (parts,), jnp.float32, smallest / len(cuts), high / len(cuts))
        return jnp.repeat(jnp.exp(steps), dims[axis_at] // parts).reshape((-1,) + (1,) * (len(dims) - axis_at - 1))

    level = one(*cuts[0])
    for cut in cuts[1:]:
        level = level * one(*cut)
    return level


def setup_inputs(seed: int = 0) -> dict:
    streams_of = jax.random.split(jax.random.key(seed), 5)
    return {
        "prior": jnp.clip(1.0 * jax.random.uniform(streams_of[0], (LABELS, NZ, NY, CX), jnp.float32) ** block_scale(streams_of[0], (LABELS, NZ, NY, CX), ((1, 8), (2, 16)), -0.2, 0.2), 0.0, 1.0),
        "levels": plant(jax.random.randint(streams_of[1], (3, NZ, NY, CX), 0, 256), jax.random.fold_in(streams_of[1], 1), 0, 255).astype(jnp.int32),
        "seeds": draw_seeds(jax.random.fold_in(streams_of[4], 71), 0),
        "bclass": plant(jax.random.randint(streams_of[3], (N_GZ, N_GY), 0, 4), jax.random.fold_in(streams_of[3], 1), 0, 3).astype(jnp.int32),
    }


BETAS = (2.0, 4.0, 6.0, 8.0)
OMEGA = 0.8
FLOOR = 0.02


def reference(prior, levels, seeds, bclass):
    cls = jnp.repeat(jnp.repeat(bclass, CZ, axis=0), CY, axis=1)[:, :, None]
    beta = jnp.zeros(cls.shape, jnp.float32)
    for index in range(4):
        beta = beta + jnp.where(cls == index, BETAS[index], 0.0).astype(jnp.float32)
    ratio = levels.astype(jnp.float32) / 255.0
    weights = FLOOR + jnp.exp(-beta[None] * ratio * ratio)
    wz, wy, wx = weights[0], weights[1], weights[2]
    shape = wz.shape
    zidx = lax.broadcasted_iota(jnp.int32, shape, 0)
    yidx = lax.broadcasted_iota(jnp.int32, shape, 1)
    xidx = lax.broadcasted_iota(jnp.int32, shape, 2)
    wz_up = jnp.where(zidx == shape[0] - 1, 0.0, wz)
    wy_up = jnp.where(yidx == shape[1] - 1, 0.0, wy)
    wx_up = jnp.where(xidx == shape[2] - 1, 0.0, wx)
    wz_dn = jnp.concatenate([jnp.zeros((1,) + shape[1:], jnp.float32), wz_up[:-1]], 0)
    wy_dn = jnp.concatenate([jnp.zeros((shape[0], 1, shape[2]), jnp.float32), wy_up[:, :-1]], 1)
    wx_dn = jnp.concatenate([jnp.zeros(shape[:2] + (1,), jnp.float32), wx_up[:, :, :-1]], 2)
    degree = wz_up + wz_dn + wy_up + wy_dn + wx_up + wx_dn
    cross_up = (zidx + 1) % CZ == 0
    cross_dn = zidx % CZ == 0
    seeded = seeds > 0

    def sweep(field, frozen, onehot):
        fpad = jnp.pad(field, ((1, 1), (0, 0), (0, 0)))
        gpad = jnp.pad(frozen, ((1, 1), (0, 0), (0, 0)))
        upper = jnp.where(cross_up, gpad[2:], fpad[2:])
        lower = jnp.where(cross_dn, gpad[:-2], fpad[:-2])
        ypad = jnp.pad(field, ((0, 0), (1, 1), (0, 0)))
        xpad = jnp.pad(field, ((0, 0), (0, 0), (1, 1)))
        total = wz_up * upper + wz_dn * lower + wy_up * ypad[:, 2:] + wy_dn * ypad[:, :-2]
        total = total + wx_up * xpad[:, :, 2:] + wx_dn * xpad[:, :, :-2]
        relaxed = (1.0 - OMEGA) * field + OMEGA * total / degree
        return jnp.where(seeded, onehot, relaxed)

    def solve_label(inputs):
        start, label = inputs
        onehot = (seeds == label + 1).astype(jnp.float32)
        field = start
        for outer in range(OUTER):
            frozen = field
            for inner in range(SWEEPS):
                field = sweep(field, frozen, onehot)
        return field

    label_ids = jnp.arange(LABELS, dtype=jnp.int32)
    return lax.map(solve_label, (prior, label_ids))
```

```python
import functools

import jax
import jax.numpy as jnp
from jax import lax
from jax.experimental import pallas as pl
from jax.experimental.pallas import tpu as pltpu
from jax.sharding import PartitionSpec as P

BETAS = (2.0, 4.0, 6.0, 8.0)
OMEGA = 0.8
FLOOR = 0.02

L = 8
NP = 16
NR = 32
HX = 128
PB = NP + 2
RB = 48
PS = 2 * RB
LS = PB * PS
MIB = 1 << 20

f32 = jnp.float32
VM = pl.BlockSpec(memory_space=pltpu.VMEM)
SM = pl.BlockSpec(memory_space=pltpu.SMEM)
ANY = pl.BlockSpec(memory_space=pl.ANY)


def lanes():
    return lax.broadcasted_iota(jnp.int32, (8, HX), 1)


def rolled(a, b):
    lane = lanes()
    pa, pb = pltpu.roll(a, 1, 1), pltpu.roll(b, 1, 1)
    na, nb = pltpu.roll(a, HX - 1, 1), pltpu.roll(b, HX - 1, 1)
    return (jnp.where(lane == HX - 1, nb, na), nb), (pa, jnp.where(lane == 0, pa, pb))


def flat(ref):
    n = 1
    for d in ref.shape[:-1]:
        n *= d
    return ref.reshape(n, ref.shape[-1])


def pack_rows(a, even, near, far, per):
    af = flat(a)
    for out, start in ((near, jnp.where(even, 38, 8)), (far, jnp.where(even, 8, 38))):

        def one(l, c):
            for r in range(2):
                for h in range(2):
                    for q in range(2):
                        base = l * LS + (8 * q + 1) * PS + h * RB + start + r
                        out[(l * 2 + r) * 2 + h, 8 * q : 8 * q + 8, :] = af[pl.ds(base, 8, stride=PS), :]
            return c

        lax.fori_loop(0, L, one, 0)


def unpack_rows(a, even, near, far):
    af = flat(a)
    for src, start in ((near, jnp.where(even, 40, 6)), (far, jnp.where(even, 6, 40))):

        def one(l, c):
            for r in range(2):
                for h in range(2):
                    for q in range(2):
                        base = l * LS + (8 * q + 1) * PS + h * RB + start + r
                        af[pl.ds(base, 8, stride=PS), :] = src[(l * 2 + r) * 2 + h, 8 * q : 8 * q + 8, :]
            return c

        lax.fori_loop(0, L, one, 0)


def pack_corners(a, zeven, near, far):
    af = flat(a)
    for out, p in ((near, jnp.where(zeven, NP, 1)), (far, jnp.where(zeven, 1, NP))):
        for h in range(2):
            for i, row in enumerate((7, 40)):
                out[h, 8 * i : 8 * i + 8, :] = af[pl.ds(p * PS + h * RB + row, L, stride=LS), :]


def unpack_corners(a, zeven, near, far):
    af = flat(a)
    for src, p in ((near, jnp.where(zeven, NP + 1, 0)), (far, jnp.where(zeven, 0, NP + 1))):
        for h in range(2):
            for i, row in enumerate((7, 40)):
                af[pl.ds(p * PS + h * RB + row, L, stride=LS), :] = src[h, 8 * i : 8 * i + 8, :]


def pack_planes(a, zeven, near, far):
    for out, p in ((near, jnp.where(zeven, NP, 1)), (far, jnp.where(zeven, 1, NP))):

        def one(l, c):
            for h in range(2):
                for r in range(0, NR, 8):
                    out[l, r : r + 8, h * HX : h * HX + HX] = a[l, p, h, 8 + r : 16 + r, :]
            return c

        lax.fori_loop(0, L, one, 0)


def unpack_planes(a, b, zeven, near, far):
    for src, p in ((near, jnp.where(zeven, NP + 1, 0)), (far, jnp.where(zeven, 0, NP + 1))):

        def one(l, c):
            for h in range(2):
                for r in range(0, NR, 8):
                    v = src[l, r : r + 8, h * HX : h * HX + HX]
                    a[l, p, h, 8 + r : 16 + r, :] = v
                    b[l, p, h, 8 + r : 16 + r, :] = v
            return c

        lax.fori_loop(0, L, one, 0)


def sweep_tile(src, dst, cf, sd, p, r0):
    co = [[cf[d, p, h, pl.ds(r0, 8), :] for h in range(2)] for d in range(6)]
    seed = [sd[p, h, pl.ds(r0, 8), :] for h in range(2)]
    rest = [jnp.where(s == 0, f32(1.0 - OMEGA), 0.0) for s in seed]
    for l in range(L):
        here = [src[l, p + 1, h, pl.ds(r0, 8), :] for h in range(2)]
        xn, xp = rolled(*here)
        for h in range(2):
            t = co[0][h] * src[l, p + 2, h, pl.ds(r0, 8), :] + co[1][h] * src[l, p, h, pl.ds(r0, 8), :]
            t = t + (co[2][h] * src[l, p + 1, h, pl.ds(r0 + 1, 8), :] + co[3][h] * src[l, p + 1, h, pl.ds(r0 - 1, 8), :])
            t = t + (co[4][h] * xn[h] + co[5][h] * xp[h])
            t = t + rest[h] * here[h]
            dst[l, p + 1, h, pl.ds(r0, 8), :] = jnp.where(seed[h] == l + 1, 1.0, t)


def wide_row(i):
    return jnp.where(i == 4, 33, 7 + 8 * i)


def sweep(src, dst, cf, sd, first, count, step, wide):
    tiles = 5 if wide else 4

    def body(i, c):
        p = first + (i // tiles) * step
        t = i % tiles
        sweep_tile(src, dst, cf, sd, p, wide_row(t) if wide else 8 + 8 * t)
        return c

    lax.fori_loop(0, count * tiles, body, 0)


def coefficients(w, sd, cf, first, count):
    def body(i, c):
        p, r0 = first + i // 5, wide_row(i % 5)
        seed = [sd[p, h, pl.ds(r0, 8), :] for h in range(2)]
        zu = [w[0, p + 1, h, pl.ds(r0, 8), :] for h in range(2)]
        zd = [w[0, p, h, pl.ds(r0, 8), :] for h in range(2)]
        yu = [w[1, p + 1, h, pl.ds(r0, 8), :] for h in range(2)]
        yd = [w[1, p + 1, h, pl.ds(r0 - 1, 8), :] for h in range(2)]
        xu = [w[2, p + 1, h, pl.ds(r0, 8), :] for h in range(2)]
        lane = lanes()
        pa, pb = (pltpu.roll(x, 1, 1) for x in xu)
        xd = [jnp.where(lane == 0, 0.0, pa), jnp.where(lane == 0, pa, pb)]
        for h in range(2):
            degree = zu[h] + zd[h] + yu[h] + yd[h] + xu[h] + xd[h]
            live = (seed[h] == 0) & (degree > 0.0)
            scale = jnp.where(live, OMEGA / jnp.where(live, degree, 1.0), 0.0)
            for d, x in enumerate((zu, zd, yu, yd, xu, xd)):
                cf[d, p, h, pl.ds(r0, 8), :] = scale * x[h]
        return c

    lax.fori_loop(0, count * 5, body, 0)


def k_load(at, bclass, prior, levels, seeds, a, w, sd, near, far, lev, sem):
    even, top_slab, top_band = at[0] == 0, at[2] == 1, at[3] == 1
    copies = []
    for h in range(2):
        cols = pl.ds(h * HX, HX)
        copies.append(pltpu.make_async_copy(levels.at[:, :, :, cols], lev.at[:, :, h], sem.at[2 * h]))
        copies.append(pltpu.make_async_copy(seeds.at[:, :, cols], sd.at[:, h, pl.ds(8, NR), :], sem.at[2 * h + 1]))
    for h in range(2):
        cols = pl.ds(h * HX, HX)
        for l in range(L):
            copies.append(
                pltpu.make_async_copy(
                    prior.at[l, :, :, cols], a.at[l, pl.ds(1, NP), h, pl.ds(8, NR), :], sem.at[4 + h * L + l]
                )
            )
    for c in copies:
        c.start()
    cls = bclass[0, 0]
    beta = f32(0.0)
    for index in range(4):
        beta = beta + jnp.where(cls == index, f32(BETAS[index]), f32(0.0))
    for c in copies[:4]:
        c.wait()
    row = lax.broadcasted_iota(jnp.int32, (8, HX), 0)
    lane = lanes()

    def weigh(i, c):
        p, t = i // 4, i % 4
        r0 = pl.multiple_of(8 * t, 8)
        for d in range(3):
            for h in range(2):
                ratio = lev[d, p, h, pl.ds(r0, 8), :].astype(f32) / 255.0
                x = FLOOR + jnp.exp(-beta * ratio * ratio)
                if d == 0:
                    x = jnp.where(top_slab & (p == NP - 1), 0.0, x)
                elif d == 1:
                    x = jnp.where((row == 7) & (top_band & (t == 3)), 0.0, x)
                elif h == 1:
                    x = jnp.where(lane == HX - 1, 0.0, x)
                w[d, p + 1, h, pl.ds(r0 + 8, 8), :] = x
        return c

    lax.fori_loop(0, NP * 4, weigh, 0)
    for c in copies[4:]:
        c.wait()
    pack_rows(a, even, near, far, 21)
    wf, sf = flat(w), flat(sd)
    for out, edge, other in (
        (near, jnp.where(even, 39, 8), jnp.where(even, 38, 9)),
        (far, jnp.where(even, 8, 39), jnp.where(even, 9, 38)),
    ):
        for h in range(2):
            for q in range(2):
                cut = slice(8 * q, 8 * q + 8)
                for i, (d, rw) in enumerate(((0, edge), (2, edge), (1, edge), (1, other))):
                    out[32 + 2 * i + h, cut, :] = wf[pl.ds((d * PB + 8 * q + 1) * PS + h * RB + rw, 8, stride=PS), :]
                out[40 + h, cut, :] = sf[pl.ds(8 * q * PS + h * RB + edge, 8, stride=PS), :].astype(f32)


def k_rows(at, near, far, a_in, w_in, sd_in, a, w, sd, cnear, cfar):
    even, zeven = at[0] == 0, at[1] == 0
    unpack_rows(a, even, near, far)
    wf, sf = flat(w), flat(sd)
    for src, edge, other in (
        (near, jnp.where(even, 40, 7), jnp.where(even, 41, 6)),
        (far, jnp.where(even, 7, 40), jnp.where(even, 6, 41)),
    ):
        for h in range(2):
            for q in range(2):
                cut = slice(8 * q, 8 * q + 8)
                for i, (d, rw) in enumerate(((0, edge), (2, edge), (1, edge), (1, other))):
                    wf[pl.ds((d * PB + 8 * q + 1) * PS + h * RB + rw, 8, stride=PS), :] = src[32 + 2 * i + h, cut, :]
                sf[pl.ds(8 * q * PS + h * RB + edge, 8, stride=PS), :] = src[40 + h, cut, :].astype(jnp.int32)
    pack_corners(a, zeven, cnear, cfar)
    for out in (cnear, cfar):
        for h in range(2):
            for t in range(5):
                r0 = 7 + 8 * t if t < 4 else 33
                out[h, r0 + 9 : r0 + 17, :] = w[0, NP, h, r0 : r0 + 8, :]


def k_inner(at, a_in, w, sd, a, b, cf):
    coefficients(w, sd, cf, 1, NP - 1)
    sweep(a, b, cf, sd, 1, NP - 2, 1, True)
    sweep(b, a, cf, sd, 2, NP - 4, 1, False)


def k_outer(at, znear, zfar, cnear, cfar, w_in, sd, a_in, b_in, cf_in, w, a, b, cf, near, far, pnear, pfar):
    even, zeven = at[0] == 0, at[1] == 0
    unpack_planes(a, b, zeven, znear, zfar)
    unpack_corners(a, zeven, cnear, cfar)
    for h in range(2):
        for t in range(5):
            r0 = 7 + 8 * t if t < 4 else 33
            cut = slice(r0 + 9, r0 + 17)
            w[0, 0, h, r0 : r0 + 8, :] = jnp.where(zeven, cfar[h, cut, :], cnear[h, cut, :])
    coefficients(w, sd, cf, 0, 1)
    sweep(a, b, cf, sd, 0, 2, NP - 1, True)
    sweep(b, a, cf, sd, 0, 2, 1, False)
    sweep(b, a, cf, sd, NP - 2, 2, 1, False)
    pack_planes(a, zeven, pnear, pfar)
    pack_rows(a, even, near, far, 16)


def k_rows2(at, near, far, a_in, a, cnear, cfar):
    even, zeven = at[0] == 0, at[1] == 0
    unpack_rows(a, even, near, far)
    pack_corners(a, zeven, cnear, cfar)


def put(a, out, sem, spans):
    copies = []
    for k, (first, count) in enumerate(spans):
        for h in range(2):
            for l in range(L):
                copies.append(
                    pltpu.make_async_copy(
                        a.at[l, pl.ds(1 + first, count), h, pl.ds(8, NR), :],
                        out.at[l, pl.ds(first, count), :, pl.ds(h * HX, HX)],
                        sem.at[(k * 2 + h) * L + l],
                    )
                )
    for c in copies:
        c.start()
    for c in copies:
        c.wait()


def k_inner2(at, a_in, b_in, cf, sd, a, b, out, sem):
    sweep(a, b, cf, sd, 1, NP - 2, 1, True)
    sweep(b, a, cf, sd, 2, NP - 4, 1, False)
    put(a, out, sem, ((2, NP - 4),))


def k_outer2(at, znear, zfar, cnear, cfar, cf, sd, a_in, b_in, out_in, a, b, out, sem):
    zeven = at[1] == 0
    unpack_planes(a, b, zeven, znear, zfar)
    unpack_corners(a, zeven, cnear, cfar)
    sweep(a, b, cf, sd, 0, 2, NP - 1, True)
    sweep(b, a, cf, sd, 0, 2, 1, False)
    sweep(b, a, cf, sd, NP - 2, 2, 1, False)
    put(a, out, sem, ((0, 2), (NP - 2, 2)))


def vmem(shape, dtype=f32):
    return pltpu.VMEM(shape, dtype)


A_SHAPE = (L, PB, 2, RB, HX)
W_SHAPE = (3, PB, 2, RB, HX)
S_SHAPE = (NP, 2, RB, HX)
C_SHAPE = (6, NP, 2, RB, HX)


def call(kernel, ins, outs, *, aliases=None, scratch=(), cost=3000000):
    specs = []
    for kind, _ in ins:
        specs.append({"s": SM, "v": VM, "a": ANY}[kind])
    return pl.pallas_call(
        kernel,
        out_shape=tuple(o for _, o in outs),
        in_specs=specs,
        out_specs=tuple({"v": VM, "a": ANY}[k] for k, _ in outs),
        input_output_aliases=aliases or {},
        scratch_shapes=list(scratch),
        name=kernel.__name__,
        cost_estimate=pl.CostEstimate(flops=cost, bytes_accessed=cost, transcendentals=0),
        compiler_params=pltpu.CompilerParams(vmem_limit_bytes=32 * MIB),
    )(*(x for _, x in ins))


def swaps(n):
    near = [(i, i ^ 1) for i in range(n)]
    far = []
    for i in range(1, n - 1, 2):
        far += [(i, i + 1), (i + 1, i)]
    return near, far


def per_device(prior, levels, seeds, bclass):
    iz, iy = lax.axis_index("gz"), lax.axis_index("gy")
    nz, ny = lax.axis_size("gz"), lax.axis_size("gy")
    at = jnp.stack([iy & 1, iz & 1, (iz == nz - 1).astype(jnp.int32), (iy == ny - 1).astype(jnp.int32)])
    znear_, zfar_ = swaps(nz)
    ynear_, yfar_ = swaps(ny)

    def zswap(near, far):
        far = lax.ppermute(far, "gz", zfar_)
        return lax.ppermute(near, "gz", znear_), far

    def yswap(near, far):
        far = lax.ppermute(far, "gy", yfar_)
        return lax.ppermute(near, "gy", ynear_), far

    sds = jax.ShapeDtypeStruct
    zeven = (iz & 1) == 0
    pn = lax.dynamic_index_in_dim(prior, jnp.where(zeven, NP - 1, 0), 1, keepdims=False)
    pf = lax.dynamic_index_in_dim(prior, jnp.where(zeven, 0, NP - 1), 1, keepdims=False)

    rows = sds((42, NP, HX), f32)
    a, w, sd, near, far = call(
        k_load,
        [("s", at), ("s", bclass), ("a", prior), ("a", levels), ("a", seeds)],
        [("v", vmem(A_SHAPE)), ("v", vmem(W_SHAPE)), ("v", vmem(S_SHAPE, jnp.int32)), ("v", rows), ("v", rows)],
        scratch=[pltpu.VMEM((3, NP, 2, NR, HX), jnp.int32), pltpu.SemaphoreType.DMA((20,))],
    )
    near, far = yswap(near, far)
    zn, zf = zswap(pn, pf)
    corner = sds((2, 56, HX), f32)
    a, w, sd, cn, cf_ = call(
        k_rows,
        [("s", at), ("v", near), ("v", far), ("v", a), ("v", w), ("v", sd)],
        [("v", vmem(A_SHAPE)), ("v", vmem(W_SHAPE)), ("v", vmem(S_SHAPE, jnp.int32)), ("v", corner), ("v", corner)],
        aliases={3: 0, 4: 1, 5: 2},
    )
    cn, cf_ = zswap(cn, cf_)
    a, b, cf = call(
        k_inner,
        [("s", at), ("v", a), ("v", w), ("v", sd)],
        [("v", vmem(A_SHAPE)), ("v", vmem(A_SHAPE)), ("v", vmem(C_SHAPE))],
        aliases={1: 0},
        cost=30000000,
    )
    plane = sds((L, NR, 2 * HX), f32)
    rows = sds((32, NP, HX), f32)
    w, a, b, cf, near, far, pn, pf = call(
        k_outer,
        [("s", at), ("v", zn), ("v", zf), ("v", cn), ("v", cf_), ("v", w), ("v", sd), ("v", a), ("v", b), ("v", cf)],
        [("v", vmem(W_SHAPE)), ("v", vmem(A_SHAPE)), ("v", vmem(A_SHAPE)), ("v", vmem(C_SHAPE))]
        + [("v", rows), ("v", rows), ("v", plane), ("v", plane)],
        aliases={5: 0, 7: 1, 8: 2, 9: 3},
    )
    near, far = yswap(near, far)
    zn, zf = zswap(pn, pf)
    corner = sds((2, 16, HX), f32)
    a, cn, cf_ = call(
        k_rows2,
        [("s", at), ("v", near), ("v", far), ("v", a)],
        [("v", vmem(A_SHAPE)), ("v", corner), ("v", corner)],
        aliases={3: 0},
    )
    cn, cf_ = zswap(cn, cf_)
    whole = sds(prior.shape, f32)
    a, b, out = call(
        k_inner2,
        [("s", at), ("v", a), ("v", b), ("v", cf), ("v", sd)],
        [("v", vmem(A_SHAPE)), ("v", vmem(A_SHAPE)), ("a", whole)],
        aliases={1: 0, 2: 1},
        scratch=[pltpu.SemaphoreType.DMA((16,))],
        cost=30000000,
    )
    a, b, out = call(
        k_outer2,
        [("s", at), ("v", zn), ("v", zf), ("v", cn), ("v", cf_), ("v", cf), ("v", sd), ("v", a), ("v", b), ("a", out)],
        [("v", vmem(A_SHAPE)), ("v", vmem(A_SHAPE)), ("a", whole)],
        aliases={7: 0, 8: 1, 9: 2},
        scratch=[pltpu.SemaphoreType.DMA((32,))],
    )
    return out


def solution(mesh):
    placed = (
        P(None, "gz", "gy", None),
        P(None, "gz", "gy", None),
        P("gz", "gy", None),
        P("gz", "gy"),
    )
    return jax.shard_map(
        per_device, mesh=mesh, in_specs=placed, out_specs=P(None, "gz", "gy", None), check_vma=False
    )
```

```python
import functools

import jax
import jax.numpy as jnp
from jax import lax
from jax.experimental import pallas as pl
from jax.experimental.pallas import tpu as pltpu
from jax.sharding import PartitionSpec as P

BETAS = (2.0, 4.0, 6.0, 8.0)
OMEGA = 0.8
FLOOR = 0.02

L = 8
NP = 16
NR = 32
HX = 128
PB = NP + 2
RB = 48
PS = 2 * RB
LS = PB * PS
MIB = 1 << 20

f32 = jnp.float32
VM = pl.BlockSpec(memory_space=pltpu.VMEM)
SM = pl.BlockSpec(memory_space=pltpu.SMEM)
ANY = pl.BlockSpec(memory_space=pltpu.HBM)


def lanes():
    return lax.broadcasted_iota(jnp.int32, (8, HX), 1)


def rolled(a, b):
    lane = lanes()
    pa, pb = pltpu.roll(a, 1, 1), pltpu.roll(b, 1, 1)
    na, nb = pltpu.roll(a, HX - 1, 1), pltpu.roll(b, HX - 1, 1)
    return (jnp.where(lane == HX - 1, nb, na), nb), (pa, jnp.where(lane == 0, pa, pb))


def flat(ref):
    n = 1
    for d in ref.shape[:-1]:
        n *= d
    return ref.reshape(n, ref.shape[-1])


def pack_rows(a, even, near, far, per):
    af = flat(a)
    for out, start in ((near, jnp.where(even, 38, 8)), (far, jnp.where(even, 8, 38))):

        def one(l, c):
            for r in range(2):
                for h in range(2):
                    for q in range(2):
                        base = l * LS + (8 * q + 1) * PS + h * RB + start + r
                        out[(l * 2 + r) * 2 + h, 8 * q : 8 * q + 8, :] = af[pl.ds(base, 8, stride=PS), :]
            return c

        lax.fori_loop(0, L, one, 0)


def unpack_rows(a, even, near, far):
    af = flat(a)
    for src, start in ((near, jnp.where(even, 40, 6)), (far, jnp.where(even, 6, 40))):

        def one(l, c):
            for r in range(2):
                for h in range(2):
                    for q in range(2):
                        base = l * LS + (8 * q + 1) * PS + h * RB + start + r
                        af[pl.ds(base, 8, stride=PS), :] = src[(l * 2 + r) * 2 + h, 8 * q : 8 * q + 8, :]
            return c

        lax.fori_loop(0, L, one, 0)


def pack_corners(a, zeven, near, far):
    af = flat(a)
    for out, p in ((near, jnp.where(zeven, NP, 1)), (far, jnp.where(zeven, 1, NP))):
        for h in range(2):
            for i, row in enumerate((7, 40)):
                out[h, 8 * i : 8 * i + 8, :] = af[pl.ds(p * PS + h * RB + row, L, stride=LS), :]


def unpack_corners(a, zeven, near, far):
    af = flat(a)
    for src, p in ((near, jnp.where(zeven, NP + 1, 0)), (far, jnp.where(zeven, 0, NP + 1))):
        for h in range(2):
            for i, row in enumerate((7, 40)):
                af[pl.ds(p * PS + h * RB + row, L, stride=LS), :] = src[h, 8 * i : 8 * i + 8, :]


def pack_planes(a, zeven, near, far):
    for out, p in ((near, jnp.where(zeven, NP, 1)), (far, jnp.where(zeven, 1, NP))):

        def one(l, c):
            for h in range(2):
                for r in range(0, NR, 8):
                    out[l, r : r + 8, h * HX : h * HX + HX] = a[l, p, h, 8 + r : 16 + r, :]
            return c

        lax.fori_loop(0, L, one, 0)


def unpack_planes(a, b, zeven, near, far):
    for src, p in ((near, jnp.where(zeven, NP + 1, 0)), (far, jnp.where(zeven, 0, NP + 1))):

        def one(l, c):
            for h in range(2):
                for r in range(0, NR, 8):
                    v = src[l, r : r + 8, h * HX : h * HX + HX]
                    a[l, p, h, 8 + r : 16 + r, :] = v
                    b[l, p, h, 8 + r : 16 + r, :] = v
            return c

        lax.fori_loop(0, L, one, 0)


def sweep(src, dst, cf, sd, first, count, step, wide, onehot):
    sf, df, kf, ef = flat(src), flat(dst), flat(cf), flat(sd)
    starts = (7, 15, 23, 31, 33) if wide else (8, 16, 24, 32)

    def body(i, c):
        p = first + i * step
        at, to = p * PS, (p + 1) * PS
        for r0 in starts:
            co = [[kf[pl.ds(at + (d * NP * 2 + h) * RB + r0, 8), :] for h in range(2)] for d in range(6)]
            seed = [ef[pl.ds(at + h * RB + r0, 8), :] for h in range(2)]
            rest = [jnp.where(s == 0, f32(1.0 - OMEGA), f32(0.0 if onehot else 1.0)) for s in seed]
            for l in range(L):
                base = to + l * LS + r0
                here = [sf[pl.ds(base + h * RB, 8), :] for h in range(2)]
                xn, xp = rolled(*here)
                for h in range(2):
                    o = base + h * RB
                    t = co[0][h] * sf[pl.ds(o + PS, 8), :] + co[1][h] * sf[pl.ds(o - PS, 8), :]
                    t = t + (co[2][h] * sf[pl.ds(o + 1, 8), :] + co[3][h] * sf[pl.ds(o - 1, 8), :])
                    t = t + (co[4][h] * xn[h] + co[5][h] * xp[h])
                    t = t + rest[h] * here[h]
                    df[pl.ds(o, 8), :] = jnp.where(seed[h] == l + 1, 1.0, t) if onehot else t
        return c

    lax.fori_loop(0, count, body, 0)


def wide_row(i):
    return jnp.where(i == 4, 33, 7 + 8 * i)


def coefficients(w, sd, cf, first, count):
    def body(i, c):
        p, r0 = first + i // 5, wide_row(i % 5)
        seed = [sd[p, h, pl.ds(r0, 8), :] for h in range(2)]
        zu = [w[0, p + 1, h, pl.ds(r0, 8), :] for h in range(2)]
        zd = [w[0, p, h, pl.ds(r0, 8), :] for h in range(2)]
        yu = [w[1, p + 1, h, pl.ds(r0, 8), :] for h in range(2)]
        yd = [w[1, p + 1, h, pl.ds(r0 - 1, 8), :] for h in range(2)]
        xu = [w[2, p + 1, h, pl.ds(r0, 8), :] for h in range(2)]
        lane = lanes()
        pa, pb = (pltpu.roll(x, 1, 1) for x in xu)
        xd = [jnp.where(lane == 0, 0.0, pa), jnp.where(lane == 0, pa, pb)]
        for h in range(2):
            degree = zu[h] + zd[h] + yu[h] + yd[h] + xu[h] + xd[h]
            live = (seed[h] == 0) & (degree > 0.0)
            scale = jnp.where(live, OMEGA / jnp.where(live, degree, 1.0), 0.0)
            for d, x in enumerate((zu, zd, yu, yd, xu, xd)):
                cf[d, p, h, pl.ds(r0, 8), :] = scale * x[h]
        return c

    lax.fori_loop(0, count * 5, body, 0)


def k_load(at, bclass, prior, levels, seeds, a, w, sd, near, far, pn, pf, lev, sem):
    even, zeven, top_slab, top_band = at[0] == 0, at[1] == 0, at[2] == 1, at[3] == 1
    copies = []
    for h in range(2):
        cols = pl.ds(h * HX, HX)
        copies.append(pltpu.make_async_copy(levels.at[:, :, :, cols], lev.at[:, :, h], sem.at[2 * h]))
        copies.append(pltpu.make_async_copy(seeds.at[:, :, cols], sd.at[:, h, pl.ds(8, NR), :], sem.at[2 * h + 1]))
    for h in range(2):
        cols = pl.ds(h * HX, HX)
        for l in range(L):
            copies.append(
                pltpu.make_async_copy(
                    prior.at[l, :, :, cols], a.at[l, pl.ds(1, NP), h, pl.ds(8, NR), :], sem.at[4 + h * L + l]
                )
            )
    copies.append(pltpu.make_async_copy(prior.at[:, jnp.where(zeven, NP - 1, 0)], pn, sem.at[20]))
    copies.append(pltpu.make_async_copy(prior.at[:, jnp.where(zeven, 0, NP - 1)], pf, sem.at[21]))
    for c in copies:
        c.start()
    cls = bclass[0, 0]
    beta = f32(0.0)
    for index in range(4):
        beta = beta + jnp.where(cls == index, f32(BETAS[index]), f32(0.0))
    for c in copies[:4]:
        c.wait()
    row = lax.broadcasted_iota(jnp.int32, (8, HX), 0)
    lane = lanes()

    def weigh(i, c):
        p, t = i // 4, i % 4
        r0 = pl.multiple_of(8 * t, 8)
        for d in range(3):
            for h in range(2):
                ratio = lev[d, p, h, pl.ds(r0, 8), :].astype(f32) / 255.0
                x = FLOOR + jnp.exp(-beta * ratio * ratio)
                if d == 0:
                    x = jnp.where(top_slab & (p == NP - 1), 0.0, x)
                elif d == 1:
                    x = jnp.where((row == 7) & (top_band & (t == 3)), 0.0, x)
                elif h == 1:
                    x = jnp.where(lane == HX - 1, 0.0, x)
                w[d, p + 1, h, pl.ds(r0 + 8, 8), :] = x
        return c

    lax.fori_loop(0, NP * 4, weigh, 0)
    for c in copies[4:]:
        c.wait()
    pack_rows(a, even, near, far, 21)
    wf, sf = flat(w), flat(sd)
    for out, edge, other in (
        (near, jnp.where(even, 39, 8), jnp.where(even, 38, 9)),
        (far, jnp.where(even, 8, 39), jnp.where(even, 9, 38)),
    ):
        for h in range(2):
            for q in range(2):
                cut = slice(8 * q, 8 * q + 8)
                for i, (d, rw) in enumerate(((0, edge), (2, edge), (1, edge), (1, other))):
                    out[32 + 2 * i + h, cut, :] = wf[pl.ds((d * PB + 8 * q + 1) * PS + h * RB + rw, 8, stride=PS), :]
                out[40 + h, cut, :] = sf[pl.ds(8 * q * PS + h * RB + edge, 8, stride=PS), :].astype(f32)


def k_rows(at, near, far, a_in, w_in, sd_in, a, w, sd, cnear, cfar):
    even, zeven = at[0] == 0, at[1] == 0
    unpack_rows(a, even, near, far)
    wf, sf = flat(w), flat(sd)
    for src, edge, other in (
        (near, jnp.where(even, 40, 7), jnp.where(even, 41, 6)),
        (far, jnp.where(even, 7, 40), jnp.where(even, 6, 41)),
    ):
        for h in range(2):
            for q in range(2):
                cut = slice(8 * q, 8 * q + 8)
                for i, (d, rw) in enumerate(((0, edge), (2, edge), (1, edge), (1, other))):
                    wf[pl.ds((d * PB + 8 * q + 1) * PS + h * RB + rw, 8, stride=PS), :] = src[32 + 2 * i + h, cut, :]
                sf[pl.ds(8 * q * PS + h * RB + edge, 8, stride=PS), :] = src[40 + h, cut, :].astype(jnp.int32)
    pack_corners(a, zeven, cnear, cfar)
    for out in (cnear, cfar):
        for h in range(2):
            for t in range(5):
                r0 = 7 + 8 * t if t < 4 else 33
                out[h, r0 + 9 : r0 + 17, :] = w[0, NP, h, r0 : r0 + 8, :]


def k_inner(at, a_in, w, sd, a, b, cf):
    coefficients(w, sd, cf, 1, NP - 1)
    sweep(a, b, cf, sd, 1, NP - 2, 1, True, True)
    sweep(b, a, cf, sd, 2, NP - 4, 1, False, False)


def k_outer(at, znear, zfar, cnear, cfar, w_in, sd, a_in, b_in, cf_in, w, a, b, cf, near, far, pnear, pfar):
    even, zeven = at[0] == 0, at[1] == 0
    unpack_planes(a, b, zeven, znear, zfar)
    unpack_corners(a, zeven, cnear, cfar)
    for h in range(2):
        for t in range(5):
            r0 = 7 + 8 * t if t < 4 else 33
            cut = slice(r0 + 9, r0 + 17)
            w[0, 0, h, r0 : r0 + 8, :] = jnp.where(zeven, cfar[h, cut, :], cnear[h, cut, :])
    coefficients(w, sd, cf, 0, 1)
    sweep(a, b, cf, sd, 0, 2, NP - 1, True, True)
    sweep(b, a, cf, sd, 0, 2, 1, False, False)
    sweep(b, a, cf, sd, NP - 2, 2, 1, False, False)
    pack_planes(a, zeven, pnear, pfar)
    pack_rows(a, even, near, far, 16)


def k_rows2(at, near, far, a_in, a, cnear, cfar):
    even, zeven = at[0] == 0, at[1] == 0
    unpack_rows(a, even, near, far)
    pack_corners(a, zeven, cnear, cfar)


def put(a, out, sem, spans):
    copies = []
    for k, (first, count) in enumerate(spans):
        for h in range(2):
            for l in range(L):
                copies.append(
                    pltpu.make_async_copy(
                        a.at[l, pl.ds(1 + first, count), h, pl.ds(8, NR), :],
                        out.at[l, pl.ds(first, count), :, pl.ds(h * HX, HX)],
                        sem.at[(k * 2 + h) * L + l],
                    )
                )
    for c in copies:
        c.start()
    for c in copies:
        c.wait()


def k_inner2(at, a_in, b_in, cf, sd, a, b, out, sem):
    sweep(a, b, cf, sd, 1, NP - 2, 1, True, False)
    sweep(b, a, cf, sd, 2, NP - 4, 1, False, False)
    put(a, out, sem, ((2, NP - 4),))


def k_outer2(at, znear, zfar, cnear, cfar, cf, sd, a_in, b_in, out_in, a, b, out, sem):
    zeven = at[1] == 0
    unpack_planes(a, b, zeven, znear, zfar)
    unpack_corners(a, zeven, cnear, cfar)
    sweep(a, b, cf, sd, 0, 2, NP - 1, True, False)
    sweep(b, a, cf, sd, 0, 2, 1, False, False)
    sweep(b, a, cf, sd, NP - 2, 2, 1, False, False)
    put(a, out, sem, ((0, 2), (NP - 2, 2)))


def vmem(shape, dtype=f32):
    return pltpu.VMEM(shape, dtype)


A_SHAPE = (L, PB, 2, RB, HX)
W_SHAPE = (3, PB, 2, RB, HX)
S_SHAPE = (NP, 2, RB, HX)
C_SHAPE = (6, NP, 2, RB, HX)


def call(kernel, ins, outs, *, aliases=None, scratch=(), cost=3000000, grant=4):
    specs = []
    for kind, _ in ins:
        specs.append({"s": SM, "v": VM, "a": ANY}[kind])
    return pl.pallas_call(
        kernel,
        out_shape=tuple(o for _, o in outs),
        in_specs=specs,
        out_specs=tuple({"v": VM, "a": ANY}[k] for k, _ in outs),
        input_output_aliases=aliases or {},
        scratch_shapes=list(scratch),
        name=kernel.__name__,
        cost_estimate=pl.CostEstimate(flops=cost, bytes_accessed=cost, transcendentals=0),
        compiler_params=pltpu.CompilerParams(vmem_limit_bytes=grant * MIB),
    )(*(x for _, x in ins))


def swaps(n):
    near = [(i, i ^ 1) for i in range(n)]
    far = []
    for i in range(1, n - 1, 2):
        far += [(i, i + 1), (i + 1, i)]
    return near, far


def per_device(prior, levels, seeds, bclass):
    iz, iy = lax.axis_index("gz"), lax.axis_index("gy")
    nz, ny = lax.axis_size("gz"), lax.axis_size("gy")
    at = jnp.stack([iy & 1, iz & 1, (iz == nz - 1).astype(jnp.int32), (iy == ny - 1).astype(jnp.int32)])
    znear_, zfar_ = swaps(nz)
    ynear_, yfar_ = swaps(ny)

    def zswap(near, far):
        far = lax.ppermute(far, "gz", zfar_)
        return lax.ppermute(near, "gz", znear_), far

    def yswap(near, far):
        far = lax.ppermute(far, "gy", yfar_)
        return lax.ppermute(near, "gy", ynear_), far

    prior, levels, seeds = (pltpu.with_memory_space_constraint(x, pltpu.HBM) for x in (prior, levels, seeds))
    sds = jax.ShapeDtypeStruct
    rows = sds((42, NP, HX), f32)
    plane = sds((L, NR, 2 * HX), f32)
    a, w, sd, near, far, pn, pf = call(
        k_load,
        [("s", at), ("s", bclass), ("a", prior), ("a", levels), ("a", seeds)],
        [("v", vmem(A_SHAPE)), ("v", vmem(W_SHAPE)), ("v", vmem(S_SHAPE, jnp.int32)), ("v", rows), ("v", rows), ("v", plane), ("v", plane)],
        scratch=[pltpu.VMEM((3, NP, 2, NR, HX), jnp.int32), pltpu.SemaphoreType.DMA((22,))],
        grant=8,
    )
    near, far = yswap(near, far)
    zn, zf = zswap(pn, pf)
    corner = sds((2, 56, HX), f32)
    a, w, sd, cn, cf_ = call(
        k_rows,
        [("s", at), ("v", near), ("v", far), ("v", a), ("v", w), ("v", sd)],
        [("v", vmem(A_SHAPE)), ("v", vmem(W_SHAPE)), ("v", vmem(S_SHAPE, jnp.int32)), ("v", corner), ("v", corner)],
        aliases={3: 0, 4: 1, 5: 2},
    )
    cn, cf_ = zswap(cn, cf_)
    a, b, cf = call(
        k_inner,
        [("s", at), ("v", a), ("v", w), ("v", sd)],
        [("v", vmem(A_SHAPE)), ("v", vmem(A_SHAPE)), ("v", vmem(C_SHAPE))],
        aliases={1: 0},
        cost=30000000,
    )
    rows = sds((32, NP, HX), f32)
    w, a, b, cf, near, far, pn, pf = call(
        k_outer,
        [("s", at), ("v", zn), ("v", zf), ("v", cn), ("v", cf_), ("v", w), ("v", sd), ("v", a), ("v", b), ("v", cf)],
        [("v", vmem(W_SHAPE)), ("v", vmem(A_SHAPE)), ("v", vmem(A_SHAPE)), ("v", vmem(C_SHAPE))]
        + [("v", rows), ("v", rows), ("v", plane), ("v", plane)],
        aliases={5: 0, 7: 1, 8: 2, 9: 3},
    )
    near, far = yswap(near, far)
    zn, zf = zswap(pn, pf)
    corner = sds((2, 16, HX), f32)
    a, cn, cf_ = call(
        k_rows2,
        [("s", at), ("v", near), ("v", far), ("v", a)],
        [("v", vmem(A_SHAPE)), ("v", corner), ("v", corner)],
        aliases={3: 0},
    )
    cn, cf_ = zswap(cn, cf_)
    whole = sds(prior.shape, f32)
    a, b, out = call(
        k_inner2,
        [("s", at), ("v", a), ("v", b), ("v", cf), ("v", sd)],
        [("v", vmem(A_SHAPE)), ("v", vmem(A_SHAPE)), ("a", whole)],
        aliases={1: 0, 2: 1},
        scratch=[pltpu.SemaphoreType.DMA((16,))],
        cost=30000000,
    )
    a, b, out = call(
        k_outer2,
        [("s", at), ("v", zn), ("v", zf), ("v", cn), ("v", cf_), ("v", cf), ("v", sd), ("v", a), ("v", b), ("a", out)],
        [("v", vmem(A_SHAPE)), ("v", vmem(A_SHAPE)), ("a", whole)],
        aliases={7: 0, 8: 1, 9: 2},
        scratch=[pltpu.SemaphoreType.DMA((32,))],
    )
    return out


def solution(mesh):
    placed = (
        P(None, "gz", "gy", None),
        P(None, "gz", "gy", None),
        P("gz", "gy", None),
        P("gz", "gy"),
    )
    return jax.shard_map(
        per_device, mesh=mesh, in_specs=placed, out_specs=P(None, "gz", "gy", None), check_vma=False
    )
```

```python
import functools

import jax
import jax.numpy as jnp
from jax import lax
from jax.experimental import pallas as pl
from jax.experimental.pallas import tpu as pltpu
from jax.sharding import PartitionSpec as P

BETAS = (2.0, 4.0, 6.0, 8.0)
OMEGA = 0.8
FLOOR = 0.02

L = 8
NP = 16
NR = 32
HX = 128
PB = NP + 2
RB = 48
PS = 2 * RB
LS = PB * PS
MIB = 1 << 20

f32 = jnp.float32
VM = pl.BlockSpec(memory_space=pltpu.VMEM)
SM = pl.BlockSpec(memory_space=pltpu.SMEM)
ANY = pl.BlockSpec(memory_space=pltpu.HBM)


def lanes():
    return lax.broadcasted_iota(jnp.int32, (8, HX), 1)


def rolled(a, b):
    lane = lanes()
    pa, pb = pltpu.roll(a, 1, 1), pltpu.roll(b, 1, 1)
    na, nb = pltpu.roll(a, HX - 1, 1), pltpu.roll(b, HX - 1, 1)
    return (jnp.where(lane == HX - 1, nb, na), nb), (pa, jnp.where(lane == 0, pa, pb))


def flat(ref):
    n = 1
    for d in ref.shape[:-1]:
        n *= d
    return ref.reshape(n, ref.shape[-1])


def pack_rows(a, even, near, far, per):
    af = flat(a)
    for out, start in ((near, jnp.where(even, 38, 8)), (far, jnp.where(even, 8, 38))):

        def one(l, c):
            for r in range(2):
                for h in range(2):
                    for q in range(2):
                        base = l * LS + (8 * q + 1) * PS + h * RB + start + r
                        out[(l * 2 + r) * 2 + h, 8 * q : 8 * q + 8, :] = af[pl.ds(base, 8, stride=PS), :]
            return c

        lax.fori_loop(0, L, one, 0)


def unpack_rows(a, even, near, far):
    af = flat(a)
    for src, start in ((near, jnp.where(even, 40, 6)), (far, jnp.where(even, 6, 40))):

        def one(l, c):
            for r in range(2):
                for h in range(2):
                    for q in range(2):
                        base = l * LS + (8 * q + 1) * PS + h * RB + start + r
                        af[pl.ds(base, 8, stride=PS), :] = src[(l * 2 + r) * 2 + h, 8 * q : 8 * q + 8, :]
            return c

        lax.fori_loop(0, L, one, 0)


def pack_corners(a, zeven, near, far):
    af = flat(a)
    for out, p in ((near, jnp.where(zeven, NP, 1)), (far, jnp.where(zeven, 1, NP))):
        for h in range(2):
            for i, row in enumerate((7, 40)):
                out[h, 8 * i : 8 * i + 8, :] = af[pl.ds(p * PS + h * RB + row, L, stride=LS), :]


def unpack_corners(a, zeven, near, far):
    af = flat(a)
    for src, p in ((near, jnp.where(zeven, NP + 1, 0)), (far, jnp.where(zeven, 0, NP + 1))):
        for h in range(2):
            for i, row in enumerate((7, 40)):
                af[pl.ds(p * PS + h * RB + row, L, stride=LS), :] = src[h, 8 * i : 8 * i + 8, :]


def pack_planes(a, zeven, near, far):
    for out, p in ((near, jnp.where(zeven, NP, 1)), (far, jnp.where(zeven, 1, NP))):

        def one(l, c):
            for h in range(2):
                for r in range(0, NR, 8):
                    out[l, r : r + 8, h * HX : h * HX + HX] = a[l, p, h, 8 + r : 16 + r, :]
            return c

        lax.fori_loop(0, L, one, 0)


def unpack_planes(a, b, zeven, near, far):
    for src, p in ((near, jnp.where(zeven, NP + 1, 0)), (far, jnp.where(zeven, 0, NP + 1))):

        def one(l, c):
            for h in range(2):
                for r in range(0, NR, 8):
                    v = src[l, r : r + 8, h * HX : h * HX + HX]
                    a[l, p, h, 8 + r : 16 + r, :] = v
                    b[l, p, h, 8 + r : 16 + r, :] = v
            return c

        lax.fori_loop(0, L, one, 0)


MID1, EDGE1 = (15, 23, 31), (7, 33)
MID2, EDGE2 = (16, 24), (8, 32)


def sweep(src, dst, cf, sd, planes, starts, onehot, group=1):
    sf, df, kf, ef = flat(src), flat(dst), flat(cf), flat(sd)
    first, count, step = planes

    def tile(p, r0):
        at, to = p * PS, (p + 1) * PS
        co = [[kf[pl.ds(at + (d * NP * 2 + h) * RB + r0, 8), :] for h in range(2)] for d in range(6)]
        seed = [ef[pl.ds(at + h * RB + r0, 8), :] for h in range(2)]
        rest = [jnp.where(s == 0, f32(1.0 - OMEGA), f32(0.0 if onehot else 1.0)) for s in seed]
        for l in range(L):
            base = to + l * LS + r0
            here = [sf[pl.ds(base + h * RB, 8), :] for h in range(2)]
            xn, xp = rolled(*here)
            for h in range(2):
                o = base + h * RB
                t = co[0][h] * sf[pl.ds(o + PS, 8), :] + co[1][h] * sf[pl.ds(o - PS, 8), :]
                t = t + (co[2][h] * sf[pl.ds(o + 1, 8), :] + co[3][h] * sf[pl.ds(o - 1, 8), :])
                t = t + (co[4][h] * xn[h] + co[5][h] * xp[h])
                t = t + rest[h] * here[h]
                df[pl.ds(o, 8), :] = jnp.where(seed[h] == l + 1, 1.0, t) if onehot else t

    def body(i, c):
        for g in range(group):
            for r0 in starts:
                tile(first + (i * group + g) * step, r0)
        return c

    lax.fori_loop(0, count // group, body, 0)


def coefficients(w, sd, cf, first, count, starts, group=1):
    wf, kf, ef = flat(w), flat(cf), flat(sd)
    lane = lanes()

    def tile(p, r0):
        seed, xu = [], []
        for h in range(2):
            seed.append(ef[pl.ds(p * PS + h * RB + r0, 8), :])
            xu.append(wf[pl.ds((2 * PB + p + 1) * PS + h * RB + r0, 8), :])
        pa, pb = (pltpu.roll(x, 1, 1) for x in xu)
        xd = [jnp.where(lane == 0, 0.0, pa), jnp.where(lane == 0, pa, pb)]
        for h in range(2):
            o = p * PS + h * RB + r0
            zd = wf[pl.ds(o, 8), :]
            zu = wf[pl.ds(o + PS, 8), :]
            yu = wf[pl.ds(o + (PB + 1) * PS, 8), :]
            yd = wf[pl.ds(o + (PB + 1) * PS - 1, 8), :]
            degree = zu + zd + yu + yd + xu[h] + xd[h]
            live = (seed[h] == 0) & (degree > 0.0)
            scale = jnp.where(live, OMEGA / jnp.where(live, degree, 1.0), 0.0)
            for d, x in enumerate((zu, zd, yu, yd, xu[h], xd[h])):
                kf[pl.ds(o + d * NP * PS, 8), :] = scale * x

    def body(i, c):
        for g in range(group):
            for r0 in starts:
                tile(first + i * group + g, r0)
        return c

    lax.fori_loop(0, count // group, body, 0)


def weigh(bclass, at, lev, w, tiles, group):
    top_slab, top_band = at[2] == 1, at[3] == 1
    cls = bclass[0, 0]
    beta = f32(0.0)
    for index in range(4):
        beta = beta + jnp.where(cls == index, f32(BETAS[index]), f32(0.0))
    row = lax.broadcasted_iota(jnp.int32, (8, HX), 0)
    lane = lanes()

    def body(i, c):
        for g in range(group):
            p = i * group + g
            for t in tiles:
                for d in range(3):
                    for h in range(2):
                        ratio = lev[d, p, h, 8 * t : 8 * t + 8, :].astype(f32) / 255.0
                        x = FLOOR + jnp.exp(-beta * ratio * ratio)
                        if d == 0:
                            x = jnp.where(top_slab & (p == NP - 1), 0.0, x)
                        elif d == 1 and t == 3:
                            x = jnp.where((row == 7) & top_band, 0.0, x)
                        elif d == 2 and h == 1:
                            x = jnp.where(lane == HX - 1, 0.0, x)
                        w[d, p + 1, h, 8 * t + 8 : 8 * t + 16, :] = x
        return c

    lax.fori_loop(0, NP // group, body, 0)


def k_load(at, bclass, prior, levels, seeds, a, w, sd, near, far, pn, pf, lev, sem):
    even, zeven = at[0] == 0, at[1] == 0
    copies = []
    for h in range(2):
        cols = pl.ds(h * HX, HX)
        copies.append(pltpu.make_async_copy(levels.at[:, :, :, cols], lev.at[:, :, h], sem.at[2 * h]))
        copies.append(pltpu.make_async_copy(seeds.at[:, :, cols], sd.at[:, h, pl.ds(8, NR), :], sem.at[2 * h + 1]))
    for h in range(2):
        cols = pl.ds(h * HX, HX)
        for l in range(L):
            copies.append(
                pltpu.make_async_copy(
                    prior.at[l, :, :, cols], a.at[l, pl.ds(1, NP), h, pl.ds(8, NR), :], sem.at[4 + h * L + l]
                )
            )
    copies.append(pltpu.make_async_copy(prior.at[:, jnp.where(zeven, NP - 1, 0)], pn, sem.at[20]))
    copies.append(pltpu.make_async_copy(prior.at[:, jnp.where(zeven, 0, NP - 1)], pf, sem.at[21]))
    for c in copies:
        c.start()
    for c in copies[:4]:
        c.wait()
    weigh(bclass, at, lev, w, (0, 3), 2)
    for c in copies[4:]:
        c.wait()
    pack_rows(a, even, near, far, 21)
    wf, sf = flat(w), flat(sd)
    for out, edge, other in (
        (near, jnp.where(even, 39, 8), jnp.where(even, 38, 9)),
        (far, jnp.where(even, 8, 39), jnp.where(even, 9, 38)),
    ):
        for h in range(2):
            for q in range(2):
                cut = slice(8 * q, 8 * q + 8)
                for i, (d, rw) in enumerate(((0, edge), (2, edge), (1, edge), (1, other))):
                    out[32 + 2 * i + h, cut, :] = wf[pl.ds((d * PB + 8 * q + 1) * PS + h * RB + rw, 8, stride=PS), :]
                out[40 + h, cut, :] = sf[pl.ds(8 * q * PS + h * RB + edge, 8, stride=PS), :].astype(f32)


def k_rows(at, near, far, a_in, w_in, sd_in, a, w, sd, cnear, cfar):
    even, zeven = at[0] == 0, at[1] == 0
    unpack_rows(a, even, near, far)
    wf, sf = flat(w), flat(sd)
    for src, edge, other in (
        (near, jnp.where(even, 40, 7), jnp.where(even, 41, 6)),
        (far, jnp.where(even, 7, 40), jnp.where(even, 6, 41)),
    ):
        for h in range(2):
            for q in range(2):
                cut = slice(8 * q, 8 * q + 8)
                for i, (d, rw) in enumerate(((0, edge), (2, edge), (1, edge), (1, other))):
                    wf[pl.ds((d * PB + 8 * q + 1) * PS + h * RB + rw, 8, stride=PS), :] = src[32 + 2 * i + h, cut, :]
                sf[pl.ds(8 * q * PS + h * RB + edge, 8, stride=PS), :] = src[40 + h, cut, :].astype(jnp.int32)
    pack_corners(a, zeven, cnear, cfar)
    for out in (cnear, cfar):
        for h in range(2):
            for t in range(5):
                r0 = 7 + 8 * t if t < 4 else 33
                out[h, r0 + 9 : r0 + 17, :] = w[0, NP, h, r0 : r0 + 8, :]


def k_mid(at, bclass, lev, a_in, w_in, sd, a, w, b, cf):
    weigh(bclass, at, lev, w, (1, 2), 2)
    coefficients(w, sd, cf, 1, NP - 1, MID1, 1)
    sweep(a, b, cf, sd, (1, NP - 2, 1), MID1, True, 2)
    sweep(b, a, cf, sd, (2, NP - 4, 1), MID2, False, 3)


def k_edge(at, a_in, b_in, cf_in, w, sd, a, b, cf):
    coefficients(w, sd, cf, 1, NP - 1, EDGE1, 3)
    sweep(a, b, cf, sd, (1, NP - 2, 1), EDGE1, True, 2)
    sweep(b, a, cf, sd, (2, NP - 4, 1), EDGE2, False, 3)


def k_outer(at, znear, zfar, cnear, cfar, w_in, sd, a_in, b_in, cf_in, w, a, b, cf, near, far, pnear, pfar):
    even, zeven = at[0] == 0, at[1] == 0
    unpack_planes(a, b, zeven, znear, zfar)
    unpack_corners(a, zeven, cnear, cfar)
    for h in range(2):
        for t in range(5):
            r0 = 7 + 8 * t if t < 4 else 33
            cut = slice(r0 + 9, r0 + 17)
            w[0, 0, h, r0 : r0 + 8, :] = jnp.where(zeven, cfar[h, cut, :], cnear[h, cut, :])
    coefficients(w, sd, cf, 0, 1, MID1 + EDGE1)
    sweep(a, b, cf, sd, (0, 2, NP - 1), MID1 + EDGE1, True)
    sweep(b, a, cf, sd, (0, 2, 1), MID2 + EDGE2, False)
    sweep(b, a, cf, sd, (NP - 2, 2, 1), MID2 + EDGE2, False)
    pack_planes(a, zeven, pnear, pfar)
    pack_rows(a, even, near, far, 16)


def k_rows2(at, near, far, a_in, a, cnear, cfar):
    even, zeven = at[0] == 0, at[1] == 0
    unpack_rows(a, even, near, far)
    pack_corners(a, zeven, cnear, cfar)


def put(a, out, sem, spans):
    copies = []
    for k, (first, count) in enumerate(spans):
        for h in range(2):
            for l in range(L):
                copies.append(
                    pltpu.make_async_copy(
                        a.at[l, pl.ds(1 + first, count), h, pl.ds(8, NR), :],
                        out.at[l, pl.ds(first, count), :, pl.ds(h * HX, HX)],
                        sem.at[(k * 2 + h) * L + l],
                    )
                )
    for c in copies:
        c.start()
    for c in copies:
        c.wait()


def k_mid2(at, a_in, b_in, cf, sd, a, b):
    sweep(a, b, cf, sd, (1, NP - 2, 1), MID1, False, 2)
    sweep(b, a, cf, sd, (2, NP - 4, 1), MID2, False, 3)


def k_edge2(at, a_in, b_in, cf, sd, a, b, out, sem):
    sweep(a, b, cf, sd, (1, NP - 2, 1), EDGE1, False, 2)
    sweep(b, a, cf, sd, (2, NP - 4, 1), EDGE2, False, 3)
    put(a, out, sem, ((2, NP - 4),))


def k_outer2(at, znear, zfar, cnear, cfar, cf, sd, a_in, b_in, out_in, a, b, out, sem):
    zeven = at[1] == 0
    unpack_planes(a, b, zeven, znear, zfar)
    unpack_corners(a, zeven, cnear, cfar)
    sweep(a, b, cf, sd, (0, 2, NP - 1), MID1 + EDGE1, False)
    sweep(b, a, cf, sd, (0, 2, 1), MID2 + EDGE2, False)
    sweep(b, a, cf, sd, (NP - 2, 2, 1), MID2 + EDGE2, False)
    put(a, out, sem, ((0, 2), (NP - 2, 2)))


def vmem(shape, dtype=f32):
    return pltpu.VMEM(shape, dtype)


A_SHAPE = (L, PB, 2, RB, HX)
W_SHAPE = (3, PB, 2, RB, HX)
S_SHAPE = (NP, 2, RB, HX)
C_SHAPE = (6, NP, 2, RB, HX)


def call(kernel, ins, outs, *, aliases=None, scratch=(), cost=3000000, grant=4):
    specs = []
    for kind, _ in ins:
        specs.append({"s": SM, "v": VM, "a": ANY}[kind])
    return pl.pallas_call(
        kernel,
        out_shape=tuple(o for _, o in outs),
        in_specs=specs,
        out_specs=tuple({"v": VM, "a": ANY}[k] for k, _ in outs),
        input_output_aliases=aliases or {},
        scratch_shapes=list(scratch),
        name=kernel.__name__,
        cost_estimate=pl.CostEstimate(flops=cost, bytes_accessed=cost, transcendentals=0),
        compiler_params=pltpu.CompilerParams(vmem_limit_bytes=grant * MIB),
    )(*(x for _, x in ins))


def swaps(n):
    near = [(i, i ^ 1) for i in range(n)]
    far = []
    for i in range(1, n - 1, 2):
        far += [(i, i + 1), (i + 1, i)]
    return near, far


def per_device(prior, levels, seeds, bclass):
    iz, iy = lax.axis_index("gz"), lax.axis_index("gy")
    nz, ny = lax.axis_size("gz"), lax.axis_size("gy")
    at = jnp.stack([iy & 1, iz & 1, (iz == nz - 1).astype(jnp.int32), (iy == ny - 1).astype(jnp.int32)])
    znear_, zfar_ = swaps(nz)
    ynear_, yfar_ = swaps(ny)

    def zswap(near, far):
        far = lax.ppermute(far, "gz", zfar_)
        return lax.ppermute(near, "gz", znear_), far

    def yswap(near, far):
        far = lax.ppermute(far, "gy", yfar_)
        return lax.ppermute(near, "gy", ynear_), far

    prior, levels, seeds = (pltpu.with_memory_space_constraint(x, pltpu.HBM) for x in (prior, levels, seeds))
    sds = jax.ShapeDtypeStruct
    rows = sds((42, NP, HX), f32)
    plane = sds((L, NR, 2 * HX), f32)
    a, w, sd, near, far, pn, pf, lev = call(
        k_load,
        [("s", at), ("s", bclass), ("a", prior), ("a", levels), ("a", seeds)],
        [("v", vmem(A_SHAPE)), ("v", vmem(W_SHAPE)), ("v", vmem(S_SHAPE, jnp.int32)), ("v", rows), ("v", rows), ("v", plane), ("v", plane)]
        + [("v", vmem((3, NP, 2, NR, HX), jnp.int32))],
        scratch=[pltpu.SemaphoreType.DMA((22,))],
    )
    near, far = yswap(near, far)
    zn, zf = zswap(pn, pf)
    a, w, b, cf = call(
        k_mid,
        [("s", at), ("s", bclass), ("v", lev), ("v", a), ("v", w), ("v", sd)],
        [("v", vmem(A_SHAPE)), ("v", vmem(W_SHAPE)), ("v", vmem(A_SHAPE)), ("v", vmem(C_SHAPE))],
        aliases={3: 0, 4: 1},
        cost=30000000,
    )
    corner = sds((2, 56, HX), f32)
    a, w, sd, cn, cf_ = call(
        k_rows,
        [("s", at), ("v", near), ("v", far), ("v", a), ("v", w), ("v", sd)],
        [("v", vmem(A_SHAPE)), ("v", vmem(W_SHAPE)), ("v", vmem(S_SHAPE, jnp.int32)), ("v", corner), ("v", corner)],
        aliases={3: 0, 4: 1, 5: 2},
    )
    cn, cf_ = zswap(cn, cf_)
    a, b, cf = call(
        k_edge,
        [("s", at), ("v", a), ("v", b), ("v", cf), ("v", w), ("v", sd)],
        [("v", vmem(A_SHAPE)), ("v", vmem(A_SHAPE)), ("v", vmem(C_SHAPE))],
        aliases={1: 0, 2: 1, 3: 2},
        cost=30000000,
    )
    rows = sds((32, NP, HX), f32)
    w, a, b, cf, near, far, pn, pf = call(
        k_outer,
        [("s", at), ("v", zn), ("v", zf), ("v", cn), ("v", cf_), ("v", w), ("v", sd), ("v", a), ("v", b), ("v", cf)],
        [("v", vmem(W_SHAPE)), ("v", vmem(A_SHAPE)), ("v", vmem(A_SHAPE)), ("v", vmem(C_SHAPE))]
        + [("v", rows), ("v", rows), ("v", plane), ("v", plane)],
        aliases={5: 0, 7: 1, 8: 2, 9: 3},
    )
    near, far = yswap(near, far)
    zn, zf = zswap(pn, pf)
    a, b = call(
        k_mid2,
        [("s", at), ("v", a), ("v", b), ("v", cf), ("v", sd)],
        [("v", vmem(A_SHAPE)), ("v", vmem(A_SHAPE))],
        aliases={1: 0, 2: 1},
        cost=30000000,
    )
    corner = sds((2, 16, HX), f32)
    a, cn, cf_ = call(
        k_rows2,
        [("s", at), ("v", near), ("v", far), ("v", a)],
        [("v", vmem(A_SHAPE)), ("v", corner), ("v", corner)],
        aliases={3: 0},
    )
    cn, cf_ = zswap(cn, cf_)
    whole = sds(prior.shape, f32)
    a, b, out = call(
        k_edge2,
        [("s", at), ("v", a), ("v", b), ("v", cf), ("v", sd)],
        [("v", vmem(A_SHAPE)), ("v", vmem(A_SHAPE)), ("a", whole)],
        aliases={1: 0, 2: 1},
        scratch=[pltpu.SemaphoreType.DMA((16,))],
        cost=30000000,
    )
    a, b, out = call(
        k_outer2,
        [("s", at), ("v", zn), ("v", zf), ("v", cn), ("v", cf_), ("v", cf), ("v", sd), ("v", a), ("v", b), ("a", out)],
        [("v", vmem(A_SHAPE)), ("v", vmem(A_SHAPE)), ("a", whole)],
        aliases={7: 0, 8: 1, 9: 2},
        scratch=[pltpu.SemaphoreType.DMA((32,))],
    )
    return out


def solution(mesh):
    placed = (
        P(None, "gz", "gy", None),
        P(None, "gz", "gy", None),
        P("gz", "gy", None),
        P("gz", "gy"),
    )
    return jax.shard_map(
        per_device, mesh=mesh, in_specs=placed, out_specs=P(None, "gz", "gy", None), check_vma=False
    )
```

```python
import jax
import jax.numpy as jnp
from jax import lax
from jax.experimental import pallas as pl
from jax.experimental.pallas import tpu as pltpu
from jax.sharding import PartitionSpec as P


BETAS = (2.0, 4.0, 6.0, 8.0)
OMEGA = 0.8
FLOOR = 0.02

L = 8
NP = 16
NR = 32
HX = 128
PB = NP + 2
RB = 48
PS = 2 * RB
LS = PB * PS
MIB = 1 << 20

f32 = jnp.float32
VM = pl.BlockSpec(memory_space=pltpu.VMEM)
SM = pl.BlockSpec(memory_space=pltpu.SMEM)
ANY = pl.BlockSpec(memory_space=pltpu.HBM)


def lanes():
    return lax.broadcasted_iota(jnp.int32, (8, HX), 1)


def rolled(a, b):
    lane = lanes()
    pa, pb = pltpu.roll(a, 1, 1), pltpu.roll(b, 1, 1)
    na, nb = pltpu.roll(a, HX - 1, 1), pltpu.roll(b, HX - 1, 1)
    return (jnp.where(lane == HX - 1, nb, na), nb), (pa, jnp.where(lane == 0, pa, pb))


def flat(ref):
    n = 1
    for d in ref.shape[:-1]:
        n *= d
    return ref.reshape(n, ref.shape[-1])


def pack_rows(a, even, near, far):
    af = flat(a)
    for out, start in ((near, jnp.where(even, 38, 8)), (far, jnp.where(even, 8, 38))):

        def one(l, c):
            for r in range(2):
                for h in range(2):
                    for q in range(2):
                        base = l * LS + (8 * q + 1) * PS + h * RB + start + r
                        out[(l * 2 + r) * 2 + h, 8 * q : 8 * q + 8, :] = af[pl.ds(base, 8, stride=PS), :]
            return c

        lax.fori_loop(0, L, one, 0)


def unpack_rows(a, even, near, far):
    af = flat(a)
    for src, start in ((near, jnp.where(even, 40, 6)), (far, jnp.where(even, 6, 40))):

        def one(l, c):
            for r in range(2):
                for h in range(2):
                    for q in range(2):
                        base = l * LS + (8 * q + 1) * PS + h * RB + start + r
                        af[pl.ds(base, 8, stride=PS), :] = src[(l * 2 + r) * 2 + h, 8 * q : 8 * q + 8, :]
            return c

        lax.fori_loop(0, L, one, 0)


def pack_planes(a, zeven, near, far):
    af = flat(a)
    for out, p in ((near, jnp.where(zeven, NP, 1)), (far, jnp.where(zeven, 1, NP))):

        def one(l, c):
            for h in range(2):
                for r in range(0, NR, 8):
                    out[pl.ds(l * NR + r, 8), h * HX : h * HX + HX] = a[l, p, h, 8 + r : 16 + r, :]
            return c

        lax.fori_loop(0, L, one, 0)
        for h in range(2):
            for i, row in enumerate((7, 40)):
                to = L * NR + 8 * i
                out[to : to + 8, h * HX : h * HX + HX] = af[pl.ds(p * PS + h * RB + row, L, stride=LS), :]


def unpack_plane(bufs, p, src):
    def one(l, c):
        for h in range(2):
            for r in range(0, NR, 8):
                v = src[pl.ds(l * NR + r, 8), h * HX : h * HX + HX]
                for buf in bufs:
                    buf[l, p, h, 8 + r : 16 + r, :] = v
        return c

    lax.fori_loop(0, L, one, 0)


CORNERS = (6, 7, 40, 41)
WIDER = (6, 14, 22, 30, 34)


def pack_corners(a, w, zeven, near, far):
    af = flat(a)
    for out, p in ((near, jnp.where(zeven, NP, 1)), (far, jnp.where(zeven, 1, NP))):
        for h in range(2):
            for i, row in enumerate(CORNERS):
                out[h, 8 * i : 8 * i + 8, :] = af[pl.ds(p * PS + h * RB + row, L, stride=LS), :]
            for r0 in WIDER:
                out[h, r0 + 26 : r0 + 34, :] = w[0, NP, h, r0 : r0 + 8, :]


def unpack_corners(a, w, zeven, near, far):
    af = flat(a)
    for src, p in ((near, jnp.where(zeven, NP + 1, 0)), (far, jnp.where(zeven, 0, NP + 1))):
        for h in range(2):
            for i, row in enumerate(CORNERS):
                af[pl.ds(p * PS + h * RB + row, L, stride=LS), :] = src[h, 8 * i : 8 * i + 8, :]
    for h in range(2):
        for r0 in WIDER:
            rows = slice(r0 + 26, r0 + 34)
            w[0, 0, h, r0 : r0 + 8, :] = jnp.where(zeven, far[h, rows, :], near[h, rows, :])


MID1, EDGE1 = (15, 23, 31), (7, 33)
MID2, EDGE2 = (16, 24), (8, 32)


def sweep(src, dst, cf, sd, planes, starts, onehot, group=1, below=None, above=None):
    sf, df, kf, ef = flat(src), flat(dst), flat(cf), flat(sd)
    lf, uf = flat(src if below is None else below), flat(src if above is None else above)
    first, count, step = planes

    def tile(p, r0):
        at, to = p * PS, (p + 1) * PS
        co = [[kf[pl.ds(at + (d * NP * 2 + h) * RB + r0, 8), :] for h in range(2)] for d in range(6)]
        seed = [ef[pl.ds(at + h * RB + r0, 8), :] for h in range(2)]
        rest = [jnp.where(s == 0, f32(1.0 - OMEGA), f32(0.0 if onehot else 1.0)) for s in seed]
        for l in range(L):
            base = to + l * LS + r0
            here = [sf[pl.ds(base + h * RB, 8), :] for h in range(2)]
            xn, xp = rolled(*here)
            for h in range(2):
                o = base + h * RB
                t = co[0][h] * uf[pl.ds(o + PS, 8), :] + co[1][h] * lf[pl.ds(o - PS, 8), :]
                t = t + (co[2][h] * sf[pl.ds(o + 1, 8), :] + co[3][h] * sf[pl.ds(o - 1, 8), :])
                t = t + (co[4][h] * xn[h] + co[5][h] * xp[h])
                t = t + rest[h] * here[h]
                df[pl.ds(o, 8), :] = jnp.where(seed[h] == l + 1, 1.0, t) if onehot else t

    def body(i, c):
        for g in range(group):
            for r0 in starts:
                tile(first + (i * group + g) * step, r0)
        return c

    lax.fori_loop(0, count // group, body, 0)


def coefficients(w, sd, cf, first, count, starts, group=1, step=1):
    wf, kf, ef = flat(w), flat(cf), flat(sd)
    lane = lanes()

    def tile(p, r0):
        seed, xu = [], []
        for h in range(2):
            seed.append(ef[pl.ds(p * PS + h * RB + r0, 8), :])
            xu.append(wf[pl.ds((2 * PB + p + 1) * PS + h * RB + r0, 8), :])
        pa, pb = (pltpu.roll(x, 1, 1) for x in xu)
        xd = [jnp.where(lane == 0, 0.0, pa), jnp.where(lane == 0, pa, pb)]
        for h in range(2):
            o = p * PS + h * RB + r0
            zd = wf[pl.ds(o, 8), :]
            zu = wf[pl.ds(o + PS, 8), :]
            yu = wf[pl.ds(o + (PB + 1) * PS, 8), :]
            yd = wf[pl.ds(o + (PB + 1) * PS - 1, 8), :]
            degree = zu + zd + yu + yd + xu[h] + xd[h]
            live = (seed[h] == 0) & (degree > 0.0)
            scale = jnp.where(live, OMEGA / jnp.where(live, degree, 1.0), 0.0)
            for d, x in enumerate((zu, zd, yu, yd, xu[h], xd[h])):
                kf[pl.ds(o + d * NP * PS, 8), :] = scale * x

    def body(i, c):
        for g in range(group):
            for r0 in starts:
                tile(first + (i * group + g) * step, r0)
        return c

    lax.fori_loop(0, count // group, body, 0)


def weigh(bclass, at, lev, w, tiles, group):
    top_slab, top_band = at[2] == 1, at[3] == 1
    cls = bclass[0, 0]
    beta = f32(0.0)
    for index in range(4):
        beta = beta + jnp.where(cls == index, f32(BETAS[index]), f32(0.0))
    row = lax.broadcasted_iota(jnp.int32, (8, HX), 0)
    lane = lanes()

    def body(i, c):
        for g in range(group):
            p = i * group + g
            for t in tiles:
                for d in range(3):
                    for h in range(2):
                        ratio = lev[d, p, h, 8 * t : 8 * t + 8, :].astype(f32) / 255.0
                        x = FLOOR + jnp.exp(-beta * ratio * ratio)
                        if d == 0:
                            x = jnp.where(top_slab & (p == NP - 1), 0.0, x)
                        elif d == 1 and t == 3:
                            x = jnp.where((row == 7) & top_band, 0.0, x)
                        elif d == 2 and h == 1:
                            x = jnp.where(lane == HX - 1, 0.0, x)
                        w[d, p + 1, h, 8 * t + 8 : 8 * t + 16, :] = x
        return c

    lax.fori_loop(0, NP // group, body, 0)


def staging(prior, levels, seeds, a, lev, sd, sem, spans):
    small, large, k = [], [], 0
    for first, count in spans:
        for h in range(2):
            cols, rows, to = pl.ds(h * HX, HX), pl.ds(first, count), pl.ds(8 + first, count)
            small.append(pltpu.make_async_copy(levels.at[:, :, rows, cols], lev.at[:, :, h, rows, :], sem.at[k]))
            small.append(pltpu.make_async_copy(seeds.at[:, rows, cols], sd.at[:, h, to, :], sem.at[k + 1]))
            large.append(pltpu.make_async_copy(prior.at[:, :, rows, cols], a.at[:, pl.ds(1, NP), h, to, :], sem.at[k + 2]))
            k += 3
    return small, large


def lines():
    return ((0, 39, 8), (2, 39, 8), (1, 39, 8), (1, 38, 9))


EXTRA = ((0, 38, 9), (2, 38, 9), (1, 37, 10))


def k_load(at, bclass, prior, levels, seeds, a, w, sd, near, far, lev, sem):
    even = at[0] == 0
    small, large = staging(prior, levels, seeds, a, lev, sd, sem, ((0, 8), (24, 8)))
    for c in small + large:
        c.start()
    for c in small:
        c.wait()
    weigh(bclass, at, lev, w, (0, 3), 2)
    for c in large:
        c.wait()
    pack_rows(a, even, near, far)
    af, wf, sf = flat(a), flat(w), flat(sd)
    for out, up in ((near, even), (far, jnp.logical_not(even))):

        def pick(hi, lo):
            return jnp.where(up, hi, lo)

        for h in range(2):
            for q in range(2):
                rows = slice(8 * q, 8 * q + 8)
                for i, (d, hi, lo) in enumerate(lines()):
                    o = (d * PB + 8 * q + 1) * PS + h * RB + pick(hi, lo)
                    out[32 + 2 * i + h, rows, :] = wf[pl.ds(o, 8, stride=PS), :]
                out[40 + h, rows, :] = sf[pl.ds(8 * q * PS + h * RB + pick(39, 8), 8, stride=PS), :].astype(f32)
        for k, p in enumerate((0, NP - 1)):
            for h in range(2):
                o = (p + 1) * PS + h * RB
                out[42 + k, 8 * h : 8 * h + 8, :] = af[pl.ds(o + pick(37, 10), L, stride=LS), :]
                for i, (d, hi, lo) in enumerate(EXTRA):
                    out[44, pl.ds((k * 2 + h) * 4 + i, 1), :] = wf[pl.ds(o + d * PB * PS + pick(hi, lo), 1), :]
                out[44, pl.ds((k * 2 + h) * 4 + 3, 1), :] = sf[pl.ds(o - PS + pick(38, 9), 1), :].astype(f32)
        for h in range(2):
            out[45, pl.ds(h, 1), :] = wf[pl.ds((NP - 1) * PS + h * RB + pick(38, 9), 1), :]


def k_mid(at, bclass, prior, levels, seeds, a_in, w_in, sd_in, a, w, sd, b, cf, pf, lev, sem, sem2):
    small, large = staging(prior, levels, seeds, a, lev, sd, sem, ((8, 16),))
    plane = jnp.where(at[1] == 0, 0, NP - 1)
    large += [pltpu.make_async_copy(prior.at[l, plane], pf.at[pl.ds(l * NR, NR), :], sem2.at[l]) for l in range(L)]
    for c in small + large:
        c.start()
    for c in small:
        c.wait()
    weigh(bclass, at, lev, w, (1, 2), 2)
    coefficients(w, sd, cf, 1, NP - 2, MID1, 1)
    for c in large:
        c.wait()
    sweep(a, b, cf, sd, (1, NP - 2, 1), MID1, True, 2)
    sweep(b, a, cf, sd, (2, NP - 4, 1), MID2, False, 3)


def k_rows(at, near, far, a_in, w_in, sd_in, a, w, sd, cnear, cfar):
    even, zeven = at[0] == 0, at[1] == 0
    unpack_rows(a, even, near, far)
    af, wf, sf = flat(a), flat(w), flat(sd)
    for src, down in ((near, jnp.logical_not(even)), (far, even)):

        def pick(hi, lo):
            return jnp.where(down, hi - NR, lo + NR)

        for h in range(2):
            for q in range(2):
                rows = slice(8 * q, 8 * q + 8)
                for i, (d, hi, lo) in enumerate(lines()):
                    o = (d * PB + 8 * q + 1) * PS + h * RB + pick(hi, lo)
                    wf[pl.ds(o, 8, stride=PS), :] = src[32 + 2 * i + h, rows, :]
                o = 8 * q * PS + h * RB + pick(39, 8)
                sf[pl.ds(o, 8, stride=PS), :] = src[40 + h, rows, :].astype(jnp.int32)
        for k, p in enumerate((0, NP - 1)):
            for h in range(2):
                o = (p + 1) * PS + h * RB
                af[pl.ds(o + pick(37, 10), L, stride=LS), :] = src[42 + k, 8 * h : 8 * h + 8, :]
                for i, (d, hi, lo) in enumerate(EXTRA):
                    wf[pl.ds(o + d * PB * PS + pick(hi, lo), 1), :] = src[44, pl.ds((k * 2 + h) * 4 + i, 1), :]
                sf[pl.ds(o - PS + pick(38, 9), 1), :] = src[44, pl.ds((k * 2 + h) * 4 + 3, 1), :].astype(jnp.int32)
        for h in range(2):
            wf[pl.ds((NP - 1) * PS + h * RB + pick(38, 9), 1), :] = src[45, pl.ds(h, 1), :]
    pack_corners(a, w, zeven, cnear, cfar)


def k_edge(at, a_in, b_in, cf_in, w, sd, a, b, cf):
    coefficients(w, sd, cf, 1, NP - 2, EDGE1, 2)
    sweep(a, b, cf, sd, (1, NP - 2, 1), EDGE1, True, 7)
    sweep(b, a, cf, sd, (2, NP - 4, 1), EDGE2, False, 6)


def k_face(at, znear, zfar, cnear, cfar, w_in, sd, a_in, b_in, cf_in, w, a, b, cf, pnear, pfar):
    zeven = at[1] == 0
    unpack_plane((a,), jnp.where(zeven, NP + 1, 0), znear)
    unpack_plane((a,), jnp.where(zeven, 0, NP + 1), zfar)
    unpack_corners(a, w, zeven, cnear, cfar)
    coefficients(w, sd, cf, 0, 2, WIDER, 1, NP - 1)
    sweep(a, b, cf, sd, (0, 2, NP - 1), WIDER, True)
    sweep(b, a, cf, sd, (0, 1, 1), MID1 + EDGE1, False, below=a)
    sweep(b, a, cf, sd, (NP - 1, 1, 1), MID1 + EDGE1, False, above=a)
    pack_planes(a, zeven, pnear, pfar)


def k_outer(at, b, cf, sd, a_in, a, near, far):
    sweep(b, a, cf, sd, (1, 2, NP - 3), MID2 + EDGE2, False)
    pack_rows(a, at[0] == 0, near, far)


def k_mid2(at, a_in, b_in, cf, sd, a, b):
    sweep(a, b, cf, sd, (1, NP - 2, 1), MID1, False, 2)
    sweep(b, a, cf, sd, (2, NP - 4, 1), MID2, False, 3)


def k_rows2(at, near, far, a_in, a):
    unpack_rows(a, at[0] == 0, near, far)


def puts(a, out, sem, first, count, spans):
    copies = []
    for k, (row, rows) in enumerate(spans):
        for h in range(2):
            copies.append(
                pltpu.make_async_copy(
                    a.at[:, pl.ds(1 + first, count), h, pl.ds(8 + row, rows), :],
                    out.at[:, pl.ds(first, count), pl.ds(row, rows), pl.ds(h * HX, HX)],
                    sem.at[2 * k + h],
                )
            )
    return copies


def k_edge2(at, a_in, b_in, cf, sd, a, b, out, sem):
    middle = puts(a, out, sem, 2, NP - 4, ((8, 16),))
    for c in middle:
        c.start()
    sweep(a, b, cf, sd, (1, NP - 2, 1), EDGE1, False, 7)
    sweep(b, a, cf, sd, (2, NP - 4, 1), EDGE2, False, 6)
    for c in middle:
        c.wait()


def finish(up, src, cf, sd, a, b):
    halo, p, beside = (jnp.where(up, hi, lo) for hi, lo in ((NP + 1, 0), (NP - 1, 0), (NP - 2, 1)))
    unpack_plane((a, b), halo, src)
    af = flat(a)
    for h in range(2):
        for i, row in enumerate((7, 40)):
            o = L * NR + 8 * i
            af[pl.ds(halo * PS + h * RB + row, L, stride=LS), :] = src[o : o + 8, h * HX : h * HX + HX]
    sweep(a, b, cf, sd, (p, 1, 1), MID1 + EDGE1, False)
    sweep(b, a, cf, sd, (p, 1, 1), MID2 + EDGE2, False)
    sweep(b, a, cf, sd, (beside, 1, 1), MID2 + EDGE2, False)


def k_near2(at, znear, cf, sd, a_in, b_in, a, b):
    finish(at[1] == 0, znear, cf, sd, a, b)


def k_far2(at, zfar, cf, sd, a_in, b_in, out_in, a, b, out, sem):
    zeven = at[1] == 0
    copies = puts(a, out, sem.at[0], 2, NP - 4, ((0, 8), (24, 8)))
    copies += puts(a, out, sem.at[1], jnp.where(zeven, NP - 2, 0), 2, ((0, NR),))
    for c in copies:
        c.start()
    finish(jnp.logical_not(zeven), zfar, cf, sd, a, b)
    copies += puts(a, out, sem.at[2], jnp.where(zeven, 0, NP - 2), 2, ((0, NR),))
    for c in copies[-2:]:
        c.start()
    for c in copies:
        c.wait()


def vmem(shape, dtype=f32):
    return pltpu.VMEM(shape, dtype)


A_SHAPE = (L, PB, 2, RB, HX)
W_SHAPE = (3, PB, 2, RB, HX)
S_SHAPE = (NP, 2, RB, HX)
C_SHAPE = (6, NP, 2, RB, HX)


def call(kernel, ins, outs, *, aliases=None, scratch=(), cost=3000000):
    return pl.pallas_call(
        kernel,
        out_shape=tuple(o for _, o in outs),
        in_specs=[{"s": SM, "v": VM, "a": ANY}[kind] for kind, _ in ins],
        out_specs=tuple({"v": VM, "a": ANY}[kind] for kind, _ in outs),
        input_output_aliases=aliases or {},
        scratch_shapes=list(scratch),
        cost_estimate=pl.CostEstimate(flops=cost, bytes_accessed=cost, transcendentals=0),
        compiler_params=pltpu.CompilerParams(vmem_limit_bytes=4 * MIB),
    )(*(x for _, x in ins))


def swaps(n):
    near = [(i, i ^ 1) for i in range(n)]
    far = [(i, (i - 1 + 2 * (i & 1)) % n) for i in range(n)]
    return near, far


def relaxed(prior, levels, seeds, bclass):
    iz, iy = lax.axis_index("gz"), lax.axis_index("gy")
    nz, ny = lax.axis_size("gz"), lax.axis_size("gy")
    at = jnp.stack([iy & 1, iz & 1, (iz == nz - 1).astype(jnp.int32), (iy == ny - 1).astype(jnp.int32)])

    def swap(name, axis, near, far):
        return one(name + "near", axis, near), one(name + "far", axis, far)

    def one(name, axis, x):
        near, far = swaps(nz if axis == "gz" else ny)
        return lax.ppermute(x, axis, near if name.endswith("near") else far)

    pn = lax.dynamic_index_in_dim(prior, jnp.where((iz & 1) == 0, NP - 1, 0), 1, keepdims=False).reshape(L * NR, 2 * HX)
    prior, levels, seeds = (pltpu.with_memory_space_constraint(x, pltpu.HBM) for x in (prior, levels, seeds))
    sds = jax.ShapeDtypeStruct
    field, weights, marks, coefs = vmem(A_SHAPE), vmem(W_SHAPE), vmem(S_SHAPE, jnp.int32), vmem(C_SHAPE)

    plane = sds((L * NR, 2 * HX), f32)
    rows = sds((46, NP, HX), f32)
    zn = one("z1near", "gz", pn)
    lev = vmem((3, NP, 2, NR, HX), jnp.int32)
    a, w, sd, near, far = call(
        k_load,
        [("s", at), ("s", bclass), ("a", prior), ("a", levels), ("a", seeds)],
        [("v", field), ("v", weights), ("v", marks), ("v", rows), ("v", rows)],
        scratch=[lev, pltpu.SemaphoreType.DMA((12,))],
    )
    near, far = swap("y1", "gy", near, far)
    a, w, sd, b, cf, pf = call(
        k_mid,
        [("s", at), ("s", bclass), ("a", prior), ("a", levels), ("a", seeds), ("v", a), ("v", w), ("v", sd)],
        [("v", field), ("v", weights), ("v", marks), ("v", field), ("v", coefs), ("v", plane)],
        aliases={5: 0, 6: 1, 7: 2},
        scratch=[lev, pltpu.SemaphoreType.DMA((6,)), pltpu.SemaphoreType.DMA((L,))],
        cost=30000000,
    )
    zf = one("z1far", "gz", pf)
    corner = sds((2, 72, HX), f32)
    a, w, sd, cn, cf_ = call(
        k_rows,
        [("s", at), ("v", near), ("v", far), ("v", a), ("v", w), ("v", sd)],
        [("v", field), ("v", weights), ("v", marks), ("v", corner), ("v", corner)],
        aliases={3: 0, 4: 1, 5: 2},
    )
    cn, cf_ = swap("c1", "gz", cn, cf_)
    a, b, cf = call(
        k_edge,
        [("s", at), ("v", a), ("v", b), ("v", cf), ("v", w), ("v", sd)],
        [("v", field), ("v", field), ("v", coefs)],
        aliases={1: 0, 2: 1, 3: 2},
        cost=30000000,
    )
    plane = sds((L * NR + 16, 2 * HX), f32)
    rows = sds((32, NP, HX), f32)
    w, a, b, cf, pn, pf = call(
        k_face,
        [("s", at), ("v", zn), ("v", zf), ("v", cn), ("v", cf_), ("v", w), ("v", sd), ("v", a), ("v", b), ("v", cf)],
        [("v", weights), ("v", field), ("v", field), ("v", coefs), ("v", plane), ("v", plane)],
        aliases={5: 0, 7: 1, 8: 2, 9: 3},
    )
    zn = one("z2near", "gz", pn)
    a, near, far = call(
        k_outer,
        [("s", at), ("v", b), ("v", cf), ("v", sd), ("v", a)],
        [("v", field), ("v", rows), ("v", rows)],
        aliases={4: 0},
    )
    near, far = swap("y2", "gy", near, far)
    zf = one("z2far", "gz", pf)
    a, b = call(
        k_mid2,
        [("s", at), ("v", a), ("v", b), ("v", cf), ("v", sd)],
        [("v", field), ("v", field)],
        aliases={1: 0, 2: 1},
        cost=30000000,
    )
    (a,) = call(k_rows2, [("s", at), ("v", near), ("v", far), ("v", a)], [("v", field)], aliases={3: 0})
    whole = sds(prior.shape, f32)
    a, b, out = call(
        k_edge2,
        [("s", at), ("v", a), ("v", b), ("v", cf), ("v", sd)],
        [("v", field), ("v", field), ("a", whole)],
        aliases={1: 0, 2: 1},
        scratch=[pltpu.SemaphoreType.DMA((2,))],
        cost=30000000,
    )
    a, b = call(
        k_near2,
        [("s", at), ("v", zn), ("v", cf), ("v", sd), ("v", a), ("v", b)],
        [("v", field), ("v", field)],
        aliases={4: 0, 5: 1},
    )
    a, b, out = call(
        k_far2,
        [("s", at), ("v", zf), ("v", cf), ("v", sd), ("v", a), ("v", b), ("a", out)],
        [("v", field), ("v", field), ("a", whole)],
        aliases={4: 0, 5: 1, 6: 2},
        scratch=[pltpu.SemaphoreType.DMA((3, 4))],
    )
    return out


def solution(mesh):
    placed = (
        P(None, "gz", "gy", None),
        P(None, "gz", "gy", None),
        P("gz", "gy", None),
        P("gz", "gy"),
    )
    return jax.shard_map(relaxed, mesh=mesh, in_specs=placed, out_specs=P(None, "gz", "gy", None), check_vma=False)
```
